32 devices in a mesh: wide: 16 (over z, y, x), rep: 2 (over core).
Axes of the slice: x: 2, y: 2, z: 4, core: 2. Of those that a mesh axis runs over, the one named last changes fastest.
Arguments:
- amplitudes: float32 [32, 32768], P('wide'), may hold values from -6 to 6
- integrals: float32 [32768, 2048], P(('wide', 'rep')), may hold values from -1.8 to 1.8
- pair_orbitals: int32 [2, 32768], P(None, 'wide'), may hold values from 0 to 1599, as said below
- occupied_energy: float32 [200], replicated, may hold values from -2 to -0.6
- virtual_energy: float32 [1600], replicated, may hold values from 0.3 to 3
Outputs:
- ladder_update: float32 [32, 32768], P('rep', 'wide')
The draws below stay inside these ranges and needn't reach their ends.
Inputs may be any that keep to these rules, and one draw needn't show every extreme that they name: `pair_orbitals`: each column names two virtual orbitals; the pairs of one sector are distinct and all of one irrep.
All inputs are finite; a program needn't handle non-finite values.
Results may differ from the reference program's by a relative error of at most 0.0003.
Values sent between devices are 32-bit elements; how exact they have to be, the bound alone decides.
A program may use at most 64 MiB of HBM per device.

```python
import jax
import jax.numpy as jnp
from jax import lax

OCC = 200
VIR = 1600
IRREPS = 8
QS = 2048
NP = 32
NQ = 32768
N_WIDE = 16


def draw_pair_orbitals(key, part):
    order = jax.random.permutation(jax.random.fold_in(key, 11), VIR).astype(jnp.int32)
    per_irrep = VIR // IRREPS
    pair_index = jnp.arange(NQ, dtype=jnp.int32)
    sector = pair_index // QS
    within = pair_index % QS
    target = sector % IRREPS
    position = sector // IRREPS * QS + within
    first_irrep = position // (per_irrep * per_irrep)
    first_slot = position // per_irrep % per_irrep
    second_slot = position % per_irrep
    first = order[first_irrep + IRREPS * first_slot]
    second = order[jnp.bitwise_xor(first_irrep, target) + IRREPS * second_slot]
    return jnp.stack([first, second], axis=0).astype(jnp.int32)


def shard_levels(own_key, dims, split, smallest, largest):
    factor_of = 1.0
    for axis_at, blocks in split:
        steps = jax.random.uniform(jax.random.fold_in(jax.random.fold_in(own_key, 6), axis_at), (blocks,), jnp.float32, smallest / len(split), largest / len(split))
        factor_of = factor_of * jnp.repeat(jnp.exp(steps), dims[axis_at] // blocks).reshape((-1,) + (1,) * (len(dims) - 1 - axis_at))
    return factor_of


def gaussian(rng, shape, spread, most, pieces=(), kind=jnp.bfloat16):
    factor_of = shard_levels(rng, shape, pieces, -0.22, 0.18) if pieces else 1.0
    result = jax.random.normal(rng, shape, jnp.float32) * spread * factor_of
    return jnp.minimum(jnp.maximum(result, -most), most).astype(kind)


def setup_inputs(seed: int = 0) -> dict:
    seeds = jax.random.split(jax.random.key(seed), 6)
    amplitudes = gaussian(seeds[0], (NP, NQ), 1.0, 6.0, ((0, 16),), jnp.float32)
    integrals = gaussian(seeds[1], (NQ, QS), 0.3, 1.8, ((0, 32),), jnp.float32)
    pair_orbitals = draw_pair_orbitals(jax.random.fold_in(seeds[5], 71), 0)
    occupied_energy = jnp.clip(jax.random.uniform(seeds[3], (OCC,), jnp.float32, -2.0, -0.6), -2.0, -0.6)
    virtual_energy = jnp.clip(jax.random.uniform(seeds[4], (VIR,), jnp.float32, 0.3, 3.0), 0.3, 3.0)
    return {"amplitudes": amplitudes, "integrals": integrals, "pair_orbitals": pair_orbitals, "occupied_energy": occupied_energy, "virtual_energy": virtual_energy}


def reference(amplitudes, integrals, pair_orbitals, occupied_energy, virtual_energy):
    pair_energy = virtual_energy[pair_orbitals[0]] + virtual_energy[pair_orbitals[1]]
    occupied_index = jnp.arange(NP, dtype=jnp.int32)
    occupied_sum = occupied_energy[occupied_index // OCC] + occupied_energy[occupied_index % OCC]

    def one_sector(sector_index):
        offset = (sector_index * QS).astype(jnp.int32)
        block_amplitudes = lax.dynamic_slice_in_dim(amplitudes, offset, QS, 1)
        block_integrals = lax.dynamic_slice_in_dim(integrals, offset, QS, 0)
        block_energy = lax.dynamic_slice_in_dim(pair_energy, offset, QS, 0)
        ladder = 0.5 * jnp.dot(block_amplitudes, block_integrals, precision=lax.Precision.HIGHEST,
                               preferred_element_type=jnp.float32)
        return ladder / (occupied_sum[:, None] - block_energy[None, :])

    blocks = lax.map(one_sector, jnp.arange(N_WIDE, dtype=jnp.int32))
    return jnp.transpose(blocks, (1, 0, 2)).reshape(NP, NQ)
```

```python
import functools

import jax
import jax.numpy as jnp
from jax import lax
from jax.experimental import pallas as pl
from jax.experimental.pallas import tpu as pltpu
from jax.sharding import PartitionSpec as P

MESH = pl.DeviceIdType.MESH
LANES = 128
K_PARTS = 1
N_PARTS = 4
DOT = 256
LOADS = 8
VMEM_BYTES = 32 << 20


def split_bf16(x):
    high = x.astype(jnp.bfloat16)
    low = (x - high.astype(jnp.float32)).astype(jnp.bfloat16)
    return high, low


def kernel(
    wide, rep, amp, integ, pairs_in, occ_in, vir_in, out,
    pairs, occ, vir, arrived, rows32, rows16, raw, high, low, index8, scale, part, other,
    send_sem, recv_sem, load_sem, own_sem, small_sem, part_send, part_recv,
):
    w, r = lax.axis_index("wide"), lax.axis_index("rep")
    own_rows, sector_pairs = amp.shape
    depth, columns = integ.shape
    total_rows = own_rows * wide
    half = total_rows // rep
    k_size, n_size, load = depth // K_PARTS, columns // N_PARTS, depth // LOADS

    across = rep - 1 - r
    barrier = pltpu.get_barrier_semaphore()
    order = list(range(1, wide))
    for d in order:
        pl.semaphore_signal(
            barrier,
            inc=1,
            device_id={"wide": lax.rem(w + d, wide), "rep": across},
            device_id_type=MESH,
        )
    for e in range(1, rep):
        pl.semaphore_signal(
            barrier, inc=1, device_id={"rep": lax.rem(r + e, rep)}, device_id_type=MESH
        )

    smalls = []
    for i, (source, held) in enumerate(((pairs_in, pairs), (occ_in, occ), (vir_in, vir))):
        smalls.append(pltpu.make_async_copy(source, held, small_sem.at[i]))
        smalls[-1].start()
    loads = []
    for i in range(LOADS):
        rows = pl.ds(i * load, load)
        loads.append(pltpu.make_async_copy(integ.at[rows], raw.at[rows], load_sem.at[i]))

    def load_all():
        for copy in loads:
            copy.start()

    pl.when(2 * w < wide)(load_all)

    def piece(target, core, k):
        start = pl.multiple_of((target * rep + core) * depth + k * k_size, k_size)
        return amp.at[:, pl.ds(start, k_size)]

    own = []
    for k in range(K_PARTS):
        own.append(pltpu.make_async_copy(piece(w, r, k), arrived.at[k, w], own_sem.at[k]))
        own[-1].start()

    pl.semaphore_wait(barrier, wide - 1 + rep - 1)
    sends = [[] for _ in range(K_PARTS)]
    for k in range(K_PARTS):
        for d in order:
            target = lax.rem(w + d, wide)
            copy = pltpu.make_async_remote_copy(
                src_ref=piece(target, across, k),
                dst_ref=arrived.at[k, w],
                send_sem=send_sem.at[k, d],
                recv_sem=recv_sem.at[k, d],
                device_id={"wide": target, "rep": across},
                device_id_type=MESH,
            )
            copy.start()
            sends[k].append(copy)

    pl.when(jnp.logical_not(2 * w < wide))(load_all)
    for copy in smalls:
        copy.wait()
    for s in range(4):
        index8[2 * s : 2 * s + 2, :] = pairs[...]
    occ_count, vir_count = occ.shape[0], vir.shape[0]
    p = r * half + lax.broadcasted_iota(jnp.int32, (half, occ_count), 0)
    lane = lax.broadcasted_iota(jnp.int32, (half, occ_count), 1)
    energies = jnp.broadcast_to(occ[...][None, :], (half, occ_count))
    first = p // occ_count
    occ_sum = jnp.sum(
        jnp.where(lane == first, energies, 0.0), axis=1, keepdims=True
    ) + jnp.sum(
        jnp.where(lane == p - first * occ_count, energies, 0.0), axis=1, keepdims=True
    )
    tables = []
    for t in range(0, vir_count, LANES):
        row = vir[t : min(t + LANES, vir_count)][None, :]
        if row.shape[1] < LANES:
            row = jnp.concatenate([row, jnp.zeros((1, LANES - row.shape[1]), row.dtype)], axis=1)
        tables.append(jnp.broadcast_to(row, (8, LANES)))
    for c in range(0, columns, LANES):
        index = index8[:, c : c + LANES]
        block, slot = index // LANES, index % LANES
        found = jnp.zeros((8, LANES), jnp.float32)
        for t, table in enumerate(tables):
            value = jnp.take_along_axis(table, slot, axis=1)
            found = jnp.where(block == t, value, found)
        vir_sum = found[0:1, :] + found[1:2, :]
        scale[:, c : c + LANES] = 0.5 / (occ_sum - vir_sum)

    for i in range(LOADS):
        loads[i].wait()
        for j in range(0, load, 16):
            rows = pl.ds(i * load + j, 16)
            h, l = split_bf16(raw[rows, :])
            high[rows, :] = h
            low[rows, :] = l

    part_copies = []

    def product(k, n):
        ns = pl.ds(n * n_size, n_size)
        total = None
        for c in range(0, k_size, DOT):
            cs = pl.ds(c, DOT)
            ks = pl.ds(k * k_size + c, DOT)
            both = jnp.dot(rows16[:, cs], high[ks, ns], preferred_element_type=jnp.float32)
            cross = jnp.dot(
                rows16[0:total_rows, cs], low[ks, ns], preferred_element_type=jnp.float32
            )
            value = both[0:total_rows] + (both[total_rows:] + cross)
            total = value if total is None else total + value
        return total

    def store(k, n, value):
        ns = pl.ds(n * n_size, n_size)
        if k:
            value = value + part[:, ns]
        part[:, ns] = value
        if k == K_PARTS - 1:
            for e in range(1, rep):
                target = lax.rem(r + e, rep)
                copy = pltpu.make_async_remote_copy(
                    src_ref=part.at[pl.ds(pl.multiple_of(target * half, 8), half), ns],
                    dst_ref=other.at[e - 1, :, ns],
                    send_sem=part_send.at[e - 1, n],
                    recv_sem=part_recv.at[e - 1, n],
                    device_id={"rep": target},
                    device_id_type=MESH,
                )
                copy.start()
                part_copies.append((n, e, copy))

    for k in range(K_PARTS):
        own[k].wait()
        for copy in sends[k]:
            copy.wait_recv()
        for s in range(wide):
            rows32[own_rows * s : own_rows * (s + 1), :] = arrived[k, s]
        h, l = split_bf16(rows32[...])
        rows16[0:total_rows, :] = h
        rows16[total_rows : 2 * total_rows, :] = l
        waiting = None
        for n in range(N_PARTS + 1):
            value = product(k, n) if n < N_PARTS else None
            if n:
                store(k, n - 1, waiting)
            waiting = value

    for n in range(N_PARTS):
        ns = pl.ds(n * n_size, n_size)
        total = part[pl.ds(pl.multiple_of(r * half, 8), half), ns]
        for m, e, copy in part_copies:
            if m == n:
                copy.wait_recv()
                total = total + other[e - 1, :, ns]
        out[:, ns] = total * scale[:, ns]

    for k in range(K_PARTS):
        for copy in sends[k]:
            copy.wait_send()
    for _, _, copy in part_copies:
        copy.wait_send()


def body(wide, rep, amplitudes, integrals, pair_orbitals, occupied_energy, virtual_energy):
    own_rows = amplitudes.shape[0]
    depth, columns = integrals.shape
    total_rows = own_rows * wide
    half = total_rows // rep
    k_size = depth // K_PARTS
    hbm = pl.BlockSpec(memory_space=pltpu.HBM)
    vmem = pl.BlockSpec(memory_space=pltpu.VMEM)
    dma = pltpu.SemaphoreType.DMA
    return pl.pallas_call(
        functools.partial(kernel, wide, rep),
        out_shape=pltpu.VMEM((half, columns), jnp.float32),
        in_specs=[hbm] * 5,
        out_specs=vmem,
        scratch_shapes=[
            pltpu.VMEM(pair_orbitals.shape, jnp.int32),
            pltpu.VMEM(occupied_energy.shape, jnp.float32),
            pltpu.VMEM(virtual_energy.shape, jnp.float32),
            pltpu.VMEM((K_PARTS, wide, own_rows, k_size), jnp.float32),
            pltpu.VMEM((total_rows, k_size), jnp.float32),
            pltpu.VMEM((2 * total_rows, k_size), jnp.bfloat16),
            pltpu.VMEM((depth, columns), jnp.float32),
            pltpu.VMEM((depth, columns), jnp.bfloat16),
            pltpu.VMEM((depth, columns), jnp.bfloat16),
            pltpu.VMEM((8, columns), jnp.int32),
            pltpu.VMEM((half, columns), jnp.float32),
            pltpu.VMEM((total_rows, columns), jnp.float32),
            pltpu.VMEM((rep - 1, half, columns), jnp.float32),
            dma((K_PARTS, wide)),
            dma((K_PARTS, wide)),
            dma((LOADS,)),
            dma((K_PARTS,)),
            dma((3,)),
            dma((rep - 1, N_PARTS)),
            dma((rep - 1, N_PARTS)),
        ],
        compiler_params=pltpu.CompilerParams(
            collective_id=0, has_side_effects=True, vmem_limit_bytes=VMEM_BYTES
        ),
    )(
        *(
            pltpu.with_memory_space_constraint(x, pltpu.HBM)
            for x in (amplitudes, integrals, pair_orbitals, occupied_energy, virtual_energy)
        )
    )


def solution(mesh):
    in_specs = (P("wide", None), P(("wide", "rep"), None), P(None, "wide"), P(), P())
    return jax.shard_map(
        functools.partial(body, mesh.shape["wide"], mesh.shape["rep"]),
        mesh=mesh,
        in_specs=in_specs,
        out_specs=P("rep", "wide"),
        check_vma=False,
    )
```

```python
import functools

import jax
import jax.numpy as jnp
from jax import lax
from jax.experimental import pallas as pl
from jax.experimental.pallas import tpu as pltpu
from jax.sharding import PartitionSpec as P

MESH = pl.DeviceIdType.MESH
LANES = 128
K_PARTS = 1
N_PARTS = 4
DOT = 256
LOADS = 8
VMEM_BYTES = 32 << 20


def split_bf16(x):
    high = x.astype(jnp.bfloat16)
    low = (x - high.astype(jnp.float32)).astype(jnp.bfloat16)
    return high, low


def kernel(
    wide, rep, amp, integ, pairs_in, occ_in, vir_in, out,
    pairs, occ, vir, arrived, rows32, rows16, raw, high, low, index8, scale, part, other,
    send_sem, recv_sem, load_sem, own_sem, small_sem, part_send, part_recv,
):
    w, r = lax.axis_index("wide"), lax.axis_index("rep")
    own_rows, sector_pairs = amp.shape
    depth, columns = integ.shape
    total_rows = own_rows * wide
    half = total_rows // rep
    k_size, n_size, load = depth // K_PARTS, columns // N_PARTS, depth // LOADS

    across = rep - 1 - r
    barrier = pltpu.get_barrier_semaphore()
    order = list(range(1, wide))
    for d in order:
        pl.semaphore_signal(
            barrier,
            inc=1,
            device_id={"wide": lax.rem(w + d, wide), "rep": across},
            device_id_type=MESH,
        )
    for e in range(1, rep):
        pl.semaphore_signal(
            barrier, inc=1, device_id={"rep": lax.rem(r + e, rep)}, device_id_type=MESH
        )

    smalls = []
    for i, (source, held) in enumerate(((pairs_in, pairs), (occ_in, occ), (vir_in, vir))):
        smalls.append(pltpu.make_async_copy(source, held, small_sem.at[i]))
        smalls[-1].start()
    loads = []
    for i in range(LOADS):
        rows = pl.ds(i * load, load)
        loads.append(pltpu.make_async_copy(integ.at[rows], raw.at[rows], load_sem.at[i]))

    def load_all():
        for copy in loads:
            copy.start()

    pl.when(2 * w < wide)(load_all)

    def piece(target, core, k):
        start = pl.multiple_of((target * rep + core) * depth + k * k_size, k_size)
        return amp.at[:, pl.ds(start, k_size)]

    own = []
    for k in range(K_PARTS):
        own.append(pltpu.make_async_copy(piece(w, r, k), arrived.at[k, w], own_sem.at[k]))
        own[-1].start()

    pl.semaphore_wait(barrier, wide - 1 + rep - 1)
    for k in range(K_PARTS):
        for d in order:
            target = lax.rem(w + d, wide)
            copy = pltpu.make_async_remote_copy(
                src_ref=piece(target, across, k),
                dst_ref=arrived.at[k, w],
                send_sem=send_sem.at[k],
                recv_sem=recv_sem.at[k],
                device_id={"wide": target, "rep": across},
                device_id_type=MESH,
            )
            copy.start()

    pl.when(jnp.logical_not(2 * w < wide))(load_all)
    for copy in smalls:
        copy.wait()
    for s in range(4):
        index8[2 * s : 2 * s + 2, :] = pairs[...]
    occ_count, vir_count = occ.shape[0], vir.shape[0]
    p = r * half + lax.broadcasted_iota(jnp.int32, (half, occ_count), 0)
    lane = lax.broadcasted_iota(jnp.int32, (half, occ_count), 1)
    energies = jnp.broadcast_to(occ[...][None, :], (half, occ_count))
    first = p // occ_count
    occ_sum = jnp.sum(
        jnp.where(lane == first, energies, 0.0), axis=1, keepdims=True
    ) + jnp.sum(
        jnp.where(lane == p - first * occ_count, energies, 0.0), axis=1, keepdims=True
    )
    tables = []
    for t in range(0, vir_count, LANES):
        row = vir[t : min(t + LANES, vir_count)][None, :]
        if row.shape[1] < LANES:
            row = jnp.concatenate([row, jnp.zeros((1, LANES - row.shape[1]), row.dtype)], axis=1)
        tables.append(jnp.broadcast_to(row, (8, LANES)))
    for c in range(0, columns, LANES):
        index = index8[:, c : c + LANES]
        block, slot = index // LANES, index % LANES
        found = jnp.zeros((8, LANES), jnp.float32)
        for t, table in enumerate(tables):
            value = jnp.take_along_axis(table, slot, axis=1)
            found = jnp.where(block == t, value, found)
        vir_sum = found[0:1, :] + found[1:2, :]
        scale[:, c : c + LANES] = 0.5 / (occ_sum - vir_sum)

    for i in range(LOADS):
        loads[i].wait()
        for j in range(0, load, 16):
            rows = pl.ds(i * load + j, 16)
            h, l = split_bf16(raw[rows, :])
            high[rows, :] = h
            low[rows, :] = l

    others = arrived.at[0, 0 : wide - 1]
    part_copies = []

    def product(k, n):
        ns = pl.ds(n * n_size, n_size)
        total = None
        for c in range(0, k_size, DOT):
            cs = pl.ds(c, DOT)
            ks = pl.ds(k * k_size + c, DOT)
            both = jnp.dot(rows16[:, cs], high[ks, ns], preferred_element_type=jnp.float32)
            cross = jnp.dot(
                rows16[0:total_rows, cs], low[ks, ns], preferred_element_type=jnp.float32
            )
            value = both[0:total_rows] + (both[total_rows:] + cross)
            total = value if total is None else total + value
        return total

    def store(k, n, value):
        ns = pl.ds(n * n_size, n_size)
        if k:
            value = value + part[:, ns]
        part[:, ns] = value
        if k == K_PARTS - 1:
            for e in range(1, rep):
                target = lax.rem(r + e, rep)
                copy = pltpu.make_async_remote_copy(
                    src_ref=part.at[pl.ds(pl.multiple_of(target * half, 8), half), ns],
                    dst_ref=other.at[e - 1, :, ns],
                    send_sem=part_send.at[e - 1, n],
                    recv_sem=part_recv.at[e - 1, n],
                    device_id={"rep": target},
                    device_id_type=MESH,
                )
                copy.start()
                part_copies.append((n, e, copy))

    for k in range(K_PARTS):
        own[k].wait()
        pltpu.make_async_copy(others, others, recv_sem.at[k]).wait()
        for s in range(wide):
            rows32[own_rows * s : own_rows * (s + 1), :] = arrived[k, s]
        h, l = split_bf16(rows32[...])
        rows16[0:total_rows, :] = h
        rows16[total_rows : 2 * total_rows, :] = l
        waiting = None
        for n in range(N_PARTS + 1):
            value = product(k, n) if n < N_PARTS else None
            if n:
                store(k, n - 1, waiting)
            waiting = value

    for k in range(K_PARTS):
        pltpu.make_async_copy(others, others, send_sem.at[k]).wait()
    for n in range(N_PARTS):
        ns = pl.ds(n * n_size, n_size)
        total = part[pl.ds(pl.multiple_of(r * half, 8), half), ns]
        for m, e, copy in part_copies:
            if m == n:
                copy.wait_recv()
                total = total + other[e - 1, :, ns]
        out[:, ns] = total * scale[:, ns]

    for _, _, copy in part_copies:
        copy.wait_send()


def body(wide, rep, amplitudes, integrals, pair_orbitals, occupied_energy, virtual_energy):
    own_rows = amplitudes.shape[0]
    depth, columns = integrals.shape
    total_rows = own_rows * wide
    half = total_rows // rep
    k_size = depth // K_PARTS
    hbm = pl.BlockSpec(memory_space=pltpu.HBM)
    vmem = pl.BlockSpec(memory_space=pltpu.VMEM)
    dma = pltpu.SemaphoreType.DMA
    return pl.pallas_call(
        functools.partial(kernel, wide, rep),
        out_shape=pltpu.VMEM((half, columns), jnp.float32),
        in_specs=[hbm] * 5,
        out_specs=vmem,
        scratch_shapes=[
            pltpu.VMEM(pair_orbitals.shape, jnp.int32),
            pltpu.VMEM(occupied_energy.shape, jnp.float32),
            pltpu.VMEM(virtual_energy.shape, jnp.float32),
            pltpu.VMEM((K_PARTS, wide, own_rows, k_size), jnp.float32),
            pltpu.VMEM((total_rows, k_size), jnp.float32),
            pltpu.VMEM((2 * total_rows, k_size), jnp.bfloat16),
            pltpu.VMEM((depth, columns), jnp.float32),
            pltpu.VMEM((depth, columns), jnp.bfloat16),
            pltpu.VMEM((depth, columns), jnp.bfloat16),
            pltpu.VMEM((8, columns), jnp.int32),
            pltpu.VMEM((half, columns), jnp.float32),
            pltpu.VMEM((total_rows, columns), jnp.float32),
            pltpu.VMEM((rep - 1, half, columns), jnp.float32),
            dma((K_PARTS,)),
            dma((K_PARTS,)),
            dma((LOADS,)),
            dma((K_PARTS,)),
            dma((3,)),
            dma((rep - 1, N_PARTS)),
            dma((rep - 1, N_PARTS)),
        ],
        compiler_params=pltpu.CompilerParams(
            collective_id=0, has_side_effects=True, vmem_limit_bytes=VMEM_BYTES
        ),
    )(
        *(
            pltpu.with_memory_space_constraint(x, pltpu.HBM)
            for x in (amplitudes, integrals, pair_orbitals, occupied_energy, virtual_energy)
        )
    )


def solution(mesh):
    in_specs = (P("wide", None), P(("wide", "rep"), None), P(None, "wide"), P(), P())
    return jax.shard_map(
        functools.partial(body, mesh.shape["wide"], mesh.shape["rep"]),
        mesh=mesh,
        in_specs=in_specs,
        out_specs=P("rep", "wide"),
        check_vma=False,
    )
```

```python
import functools

import jax
import jax.numpy as jnp
from jax import lax
from jax.experimental import pallas as pl
from jax.experimental.pallas import tpu as pltpu
from jax.sharding import PartitionSpec as P

MESH = pl.DeviceIdType.MESH
LANES = 128
K_PARTS = 1
N_PARTS = 4
DOT = 256
LOADS = 8
VMEM_BYTES = 32 << 20


def split_bf16(x):
    high = x.astype(jnp.bfloat16)
    low = (x - high.astype(jnp.float32)).astype(jnp.bfloat16)
    return high, low


def kernel(
    wide, rep, amp, integ, pairs_in, occ_in, vir_in, out,
    pairs, occ, vir, arrived, rows32, rows16, raw, high, low, index8, scale, part, other,
    send_sem, recv_sem, early_sem, up_sem, load_sem, own_sem, small_sem, part_send, part_recv,
):
    w, r = lax.axis_index("wide"), lax.axis_index("rep")
    own_rows, sector_pairs = amp.shape
    depth, columns = integ.shape
    total_rows = own_rows * wide
    half = total_rows // rep
    k_size, n_size, load = depth // K_PARTS, columns // N_PARTS, depth // LOADS

    speaker = rep - 1
    across = rep - 1 - r
    edge = 3 * wide // 4
    near = (w > 0) & (w < edge)
    early = near & (r == speaker)
    barrier = pltpu.get_barrier_semaphore()

    def signal(sem, chip, core):
        pl.semaphore_signal(
            sem, inc=1, device_id={"wide": chip, "rep": core}, device_id_type=MESH
        )

    @pl.when(w == 0)
    def _():
        for j in range(1, edge):
            signal(barrier, j, speaker)

    order = list(range(1, wide))
    for d in order:
        j = lax.rem(w + d, wide)
        signal(barrier, j, jnp.where((j > 0) & (j < edge), rep - 1 - speaker, across))

    @pl.when(jnp.logical_not(near) | (r == speaker))
    def _():
        for e in range(1, rep):
            signal(barrier, w, lax.rem(r + e, rep))

    smalls = []
    for i, (source, held) in enumerate(((pairs_in, pairs), (occ_in, occ), (vir_in, vir))):
        smalls.append(pltpu.make_async_copy(source, held, small_sem.at[i]))
        smalls[-1].start()
    loads = []
    for i in range(LOADS):
        rows = pl.ds(i * load, load)
        loads.append(pltpu.make_async_copy(integ.at[rows], raw.at[rows], load_sem.at[i]))

    def load_all():
        for copy in loads:
            copy.start()

    pl.when(2 * w < wide)(load_all)

    def piece(target, core, k):
        start = pl.multiple_of((target * rep + core) * depth + k * k_size, k_size)
        return amp.at[:, pl.ds(start, k_size)]

    own = []
    for k in range(K_PARTS):
        own.append(pltpu.make_async_copy(piece(w, r, k), arrived.at[k, w], own_sem.at[k]))
        own[-1].start()

    def transfer(target, core, send):
        return pltpu.make_async_remote_copy(
            src_ref=piece(target, core, 0),
            dst_ref=arrived.at[0, w],
            send_sem=send,
            recv_sem=recv_sem.at[0],
            device_id={"wide": target, "rep": core},
            device_id_type=MESH,
        )

    @pl.when(early)
    def _():
        pl.semaphore_wait(barrier, rep)
        for e in range(rep):
            transfer(0, e, early_sem.at[e]).start()

    def exchange():
        pl.semaphore_wait(barrier, wide - 1 + rep - 1)
        for d in order:
            transfer(lax.rem(w + d, wide), across, send_sem.at[0]).start()

    def exchange_near():
        @pl.when(early)
        def _():
            pl.semaphore_wait(up_sem, 1)

        @pl.when(jnp.logical_not(early))
        def _():
            pl.semaphore_wait(barrier, (wide - 1) * rep + 1)
            signal(up_sem, w, speaker)

        for d in range(1, wide - 1):
            target = w + d
            target = jnp.where(target >= wide, target - wide + 1, target)
            transfer(target, across, send_sem.at[0]).start()

    pl.when(w >= edge)(exchange)
    pl.when(near)(exchange_near)
    pl.when(2 * w >= wide)(load_all)

    for copy in smalls:
        copy.wait()
    for s in range(4):
        index8[2 * s : 2 * s + 2, :] = pairs[...]
    occ_count, vir_count = occ.shape[0], vir.shape[0]
    p = r * half + lax.broadcasted_iota(jnp.int32, (half, occ_count), 0)
    lane = lax.broadcasted_iota(jnp.int32, (half, occ_count), 1)
    energies = jnp.broadcast_to(occ[...][None, :], (half, occ_count))
    first = p // occ_count
    occ_sum = jnp.sum(
        jnp.where(lane == first, energies, 0.0), axis=1, keepdims=True
    ) + jnp.sum(
        jnp.where(lane == p - first * occ_count, energies, 0.0), axis=1, keepdims=True
    )
    tables = []
    for t in range(0, vir_count, LANES):
        row = vir[t : min(t + LANES, vir_count)][None, :]
        if row.shape[1] < LANES:
            row = jnp.concatenate([row, jnp.zeros((1, LANES - row.shape[1]), row.dtype)], axis=1)
        tables.append(jnp.broadcast_to(row, (8, LANES)))
    for c in range(0, columns, LANES):
        index = index8[:, c : c + LANES]
        block, slot = index // LANES, index % LANES
        found = jnp.zeros((8, LANES), jnp.float32)
        for t, table in enumerate(tables):
            value = jnp.take_along_axis(table, slot, axis=1)
            found = jnp.where(block == t, value, found)
        vir_sum = found[0:1, :] + found[1:2, :]
        scale[:, c : c + LANES] = 0.5 / (occ_sum - vir_sum)

    for i in range(LOADS):
        loads[i].wait()
        for j in range(0, load, 16):
            rows = pl.ds(i * load + j, 16)
            h, l = split_bf16(raw[rows, :])
            high[rows, :] = h
            low[rows, :] = l

    pl.when(w == 0)(exchange)
    others = arrived.at[0, 0 : wide - 1]
    part_copies = []

    def product(k, n):
        ns = pl.ds(n * n_size, n_size)
        total = None
        for c in range(0, k_size, DOT):
            cs = pl.ds(c, DOT)
            ks = pl.ds(k * k_size + c, DOT)
            both = jnp.dot(rows16[:, cs], high[ks, ns], preferred_element_type=jnp.float32)
            cross = jnp.dot(
                rows16[0:total_rows, cs], low[ks, ns], preferred_element_type=jnp.float32
            )
            value = both[0:total_rows] + (both[total_rows:] + cross)
            total = value if total is None else total + value
        return total

    def store(k, n, value):
        ns = pl.ds(n * n_size, n_size)
        if k:
            value = value + part[:, ns]
        part[:, ns] = value
        if k == K_PARTS - 1:
            for e in range(1, rep):
                target = lax.rem(r + e, rep)
                copy = pltpu.make_async_remote_copy(
                    src_ref=part.at[pl.ds(pl.multiple_of(target * half, 8), half), ns],
                    dst_ref=other.at[e - 1, :, ns],
                    send_sem=part_send.at[e - 1, n],
                    recv_sem=part_recv.at[e - 1, n],
                    device_id={"rep": target},
                    device_id_type=MESH,
                )
                copy.start()
                part_copies.append((n, e, copy))

    for k in range(K_PARTS):
        own[k].wait()
        pltpu.make_async_copy(others, others, recv_sem.at[k]).wait()
        for s in range(wide):
            rows32[own_rows * s : own_rows * (s + 1), :] = arrived[k, s]
        h, l = split_bf16(rows32[...])
        rows16[0:total_rows, :] = h
        rows16[total_rows : 2 * total_rows, :] = l
        waiting = None
        for n in range(N_PARTS + 1):
            value = product(k, n) if n < N_PARTS else None
            if n:
                store(k, n - 1, waiting)
            waiting = value

    for k in range(K_PARTS):
        fewer = arrived.at[0, 0 : wide - 2]

        @pl.when(near)
        def _():
            pltpu.make_async_copy(fewer, fewer, send_sem.at[k]).wait()

        @pl.when(jnp.logical_not(near))
        def _():
            pltpu.make_async_copy(others, others, send_sem.at[k]).wait()

    @pl.when(early)
    def _():
        for e in range(rep):
            transfer(0, e, early_sem.at[e]).wait_send()

    for n in range(N_PARTS):
        ns = pl.ds(n * n_size, n_size)
        total = part[pl.ds(pl.multiple_of(r * half, 8), half), ns]
        for m, e, copy in part_copies:
            if m == n:
                copy.wait_recv()
                total = total + other[e - 1, :, ns]
        out[:, ns] = total * scale[:, ns]

    for _, _, copy in part_copies:
        copy.wait_send()


def body(wide, rep, amplitudes, integrals, pair_orbitals, occupied_energy, virtual_energy):
    own_rows = amplitudes.shape[0]
    depth, columns = integrals.shape
    total_rows = own_rows * wide
    half = total_rows // rep
    k_size = depth // K_PARTS
    hbm = pl.BlockSpec(memory_space=pltpu.HBM)
    vmem = pl.BlockSpec(memory_space=pltpu.VMEM)
    dma = pltpu.SemaphoreType.DMA
    return pl.pallas_call(
        functools.partial(kernel, wide, rep),
        out_shape=pltpu.VMEM((half, columns), jnp.float32),
        in_specs=[hbm] * 5,
        out_specs=vmem,
        scratch_shapes=[
            pltpu.VMEM(pair_orbitals.shape, jnp.int32),
            pltpu.VMEM(occupied_energy.shape, jnp.float32),
            pltpu.VMEM(virtual_energy.shape, jnp.float32),
            pltpu.VMEM((K_PARTS, wide, own_rows, k_size), jnp.float32),
            pltpu.VMEM((total_rows, k_size), jnp.float32),
            pltpu.VMEM((2 * total_rows, k_size), jnp.bfloat16),
            pltpu.VMEM((depth, columns), jnp.float32),
            pltpu.VMEM((depth, columns), jnp.bfloat16),
            pltpu.VMEM((depth, columns), jnp.bfloat16),
            pltpu.VMEM((8, columns), jnp.int32),
            pltpu.VMEM((half, columns), jnp.float32),
            pltpu.VMEM((total_rows, columns), jnp.float32),
            pltpu.VMEM((rep - 1, half, columns), jnp.float32),
            dma((K_PARTS,)),
            dma((K_PARTS,)),
            dma((rep,)),
            pltpu.SemaphoreType.REGULAR,
            dma((LOADS,)),
            dma((K_PARTS,)),
            dma((3,)),
            dma((rep - 1, N_PARTS)),
            dma((rep - 1, N_PARTS)),
        ],
        compiler_params=pltpu.CompilerParams(
            collective_id=0, has_side_effects=True, vmem_limit_bytes=VMEM_BYTES
        ),
    )(
        *(
            pltpu.with_memory_space_constraint(x, pltpu.HBM)
            for x in (amplitudes, integrals, pair_orbitals, occupied_energy, virtual_energy)
        )
    )


def solution(mesh):
    in_specs = (P("wide", None), P(("wide", "rep"), None), P(None, "wide"), P(), P())
    return jax.shard_map(
        functools.partial(body, mesh.shape["wide"], mesh.shape["rep"]),
        mesh=mesh,
        in_specs=in_specs,
        out_specs=P("rep", "wide"),
        check_vma=False,
    )
```

```python
import functools

import jax
import jax.numpy as jnp
from jax import lax
from jax.experimental import pallas as pl
from jax.experimental.pallas import tpu as pltpu
from jax.sharding import PartitionSpec as P

MESH = pl.DeviceIdType.MESH
LANES = 128
K_PARTS = 1
N_PARTS = 4
DOT = 256
LOADS = 4
VMEM_BYTES = 32 << 20


def split_bf16(x):
    high = x.astype(jnp.bfloat16)
    low = (x - high.astype(jnp.float32)).astype(jnp.bfloat16)
    return high, low


def kernel(
    wide, rep, amp, integ, pairs_in, occ_in, vir_in, out,
    pairs, occ, vir, arrived, rows32, rows16, raw, high, low, index8, scale, part, other,
    send_sem, recv_sem, early_sem, up_sem, load_sem, own_sem, small_sem, part_send, part_recv,
):
    w, r = lax.axis_index("wide"), lax.axis_index("rep")
    own_rows, sector_pairs = amp.shape
    depth, columns = integ.shape
    total_rows = own_rows * wide
    half = total_rows // rep
    k_size, n_size, load = depth // K_PARTS, columns // N_PARTS, depth // LOADS

    across = rep - 1 - r
    early = (w > 0) & (r == 0)
    barrier = pltpu.get_barrier_semaphore()

    def signal(sem, chip, core):
        pl.semaphore_signal(
            sem, inc=1, device_id={"wide": chip, "rep": core}, device_id_type=MESH
        )

    @pl.when(w == 0)
    def _():
        for j in range(1, wide):
            signal(barrier, j, 0)

    order = list(range(1, wide))
    for d in order:
        j = lax.rem(w + d, wide)
        signal(barrier, j, jnp.where(j > 0, rep - 1, across))

    @pl.when((w == 0) | early)
    def _():
        signal(barrier, w, across)

    smalls = []
    for i, (source, held) in enumerate(((pairs_in, pairs), (occ_in, occ), (vir_in, vir))):
        smalls.append(pltpu.make_async_copy(source, held, small_sem.at[i]))
        smalls[-1].start()
    loads = []
    for i in range(LOADS):
        rows = pl.ds(i * load, load)
        loads.append(pltpu.make_async_copy(integ.at[rows], raw.at[rows], load_sem.at[i]))

    def load_all():
        for copy in loads:
            copy.start()

    load_all()

    def piece(target, core, k):
        start = pl.multiple_of((target * rep + core) * depth + k * k_size, k_size)
        return amp.at[:, pl.ds(start, k_size)]

    own = []
    for k in range(K_PARTS):
        own.append(pltpu.make_async_copy(piece(w, r, k), arrived.at[k, w], own_sem.at[k]))
        own[-1].start()

    def transfer(target, core, send):
        return pltpu.make_async_remote_copy(
            src_ref=piece(target, core, 0),
            dst_ref=arrived.at[0, w],
            send_sem=send,
            recv_sem=recv_sem.at[0],
            device_id={"wide": target, "rep": core},
            device_id_type=MESH,
        )

    @pl.when(early)
    def _():
        pl.semaphore_wait(barrier, rep)
        for e in range(rep):
            transfer(0, e, early_sem.at[e]).start()

    def exchange():
        pl.semaphore_wait(barrier, wide - 1 + rep - 1)
        for d in order:
            transfer(lax.rem(w + d, wide), across, send_sem.at[0]).start()

    def exchange_near():
        @pl.when(early)
        def _():
            pl.semaphore_wait(up_sem, 1)

        @pl.when(jnp.logical_not(early))
        def _():
            pl.semaphore_wait(barrier, (wide - 1) * rep + 1)
            signal(up_sem, w, across)

        for d in range(1, wide - 1):
            target = w + d
            target = jnp.where(target >= wide, target - wide + 1, target)
            transfer(target, across, send_sem.at[0]).start()

    pl.when(w == 0)(exchange)
    pl.when(w > 0)(exchange_near)

    for copy in smalls:
        copy.wait()
    for s in range(4):
        index8[2 * s : 2 * s + 2, :] = pairs[...]
    occ_count, vir_count = occ.shape[0], vir.shape[0]
    p = r * half + lax.broadcasted_iota(jnp.int32, (half, occ_count), 0)
    lane = lax.broadcasted_iota(jnp.int32, (half, occ_count), 1)
    energies = jnp.broadcast_to(occ[...][None, :], (half, occ_count))
    first = p // occ_count
    occ_sum = jnp.sum(
        jnp.where(lane == first, energies, 0.0), axis=1, keepdims=True
    ) + jnp.sum(
        jnp.where(lane == p - first * occ_count, energies, 0.0), axis=1, keepdims=True
    )
    tables = []
    for t in range(0, vir_count, LANES):
        row = vir[t : min(t + LANES, vir_count)][None, :]
        if row.shape[1] < LANES:
            row = jnp.concatenate([row, jnp.zeros((1, LANES - row.shape[1]), row.dtype)], axis=1)
        tables.append(jnp.broadcast_to(row, (8, LANES)))
    for c in range(0, columns, LANES):
        index = index8[:, c : c + LANES]
        block, slot = index // LANES, index % LANES
        found = jnp.zeros((8, LANES), jnp.float32)
        for t, table in enumerate(tables):
            value = jnp.take_along_axis(table, slot, axis=1)
            found = jnp.where(block == t, value, found)
        vir_sum = found[0:1, :] + found[1:2, :]
        scale[:, c : c + LANES] = 0.5 / (occ_sum - vir_sum)

    for i in range(LOADS):
        loads[i].wait()
        for j in range(0, load, 16):
            rows = pl.ds(i * load + j, 16)
            h, l = split_bf16(raw[rows, :])
            high[rows, :] = h
            low[rows, :] = l

    others = arrived.at[0, 0 : wide - 1]
    part_copies = []

    def product(k, n):
        ns = pl.ds(n * n_size, n_size)
        total = None
        for c in range(0, k_size, DOT):
            cs = pl.ds(c, DOT)
            ks = pl.ds(k * k_size + c, DOT)
            both = jnp.dot(rows16[:, cs], high[ks, ns], preferred_element_type=jnp.float32)
            cross = jnp.dot(
                rows16[0:total_rows, cs], low[ks, ns], preferred_element_type=jnp.float32
            )
            value = both[0:total_rows] + (both[total_rows:] + cross)
            total = value if total is None else total + value
        return total

    def store(k, n, value):
        ns = pl.ds(n * n_size, n_size)
        if k:
            value = value + part[:, ns]
        part[:, ns] = value
        if k == K_PARTS - 1:
            for e in range(1, rep):
                target = lax.rem(r + e, rep)
                copy = pltpu.make_async_remote_copy(
                    src_ref=part.at[pl.ds(pl.multiple_of(target * half, 8), half), ns],
                    dst_ref=other.at[e - 1, :, ns],
                    send_sem=part_send.at[e - 1, n],
                    recv_sem=part_recv.at[e - 1, n],
                    device_id={"rep": target},
                    device_id_type=MESH,
                )
                copy.start()
                part_copies.append((n, e, copy))

    for k in range(K_PARTS):
        own[k].wait()
        pltpu.make_async_copy(others, others, recv_sem.at[k]).wait()
        for s in range(wide):
            rows32[own_rows * s : own_rows * (s + 1), :] = arrived[k, s]
        h, l = split_bf16(rows32[...])
        rows16[0:total_rows, :] = h
        rows16[total_rows : 2 * total_rows, :] = l
        waiting = None
        for n in range(N_PARTS + 1):
            value = product(k, n) if n < N_PARTS else None
            if n:
                store(k, n - 1, waiting)
            waiting = value

    for k in range(K_PARTS):
        fewer = arrived.at[0, 0 : wide - 2]

        @pl.when(w > 0)
        def _():
            pltpu.make_async_copy(fewer, fewer, send_sem.at[k]).wait()

        @pl.when(w == 0)
        def _():
            pltpu.make_async_copy(others, others, send_sem.at[k]).wait()

    @pl.when(early)
    def _():
        for e in range(rep):
            transfer(0, e, early_sem.at[e]).wait_send()

    for n in range(N_PARTS):
        ns = pl.ds(n * n_size, n_size)
        total = part[pl.ds(pl.multiple_of(r * half, 8), half), ns]
        for m, e, copy in part_copies:
            if m == n:
                copy.wait_recv()
                total = total + other[e - 1, :, ns]
        out[:, ns] = total * scale[:, ns]

    for _, _, copy in part_copies:
        copy.wait_send()


def body(wide, rep, amplitudes, integrals, pair_orbitals, occupied_energy, virtual_energy):
    own_rows = amplitudes.shape[0]
    depth, columns = integrals.shape
    total_rows = own_rows * wide
    half = total_rows // rep
    k_size = depth // K_PARTS
    hbm = pl.BlockSpec(memory_space=pltpu.HBM)
    vmem = pl.BlockSpec(memory_space=pltpu.VMEM)
    dma = pltpu.SemaphoreType.DMA
    return pl.pallas_call(
        functools.partial(kernel, wide, rep),
        out_shape=pltpu.VMEM((half, columns), jnp.float32),
        in_specs=[hbm] * 5,
        out_specs=vmem,
        scratch_shapes=[
            pltpu.VMEM(pair_orbitals.shape, jnp.int32),
            pltpu.VMEM(occupied_energy.shape, jnp.float32),
            pltpu.VMEM(virtual_energy.shape, jnp.float32),
            pltpu.VMEM((K_PARTS, wide, own_rows, k_size), jnp.float32),
            pltpu.VMEM((total_rows, k_size), jnp.float32),
            pltpu.VMEM((2 * total_rows, k_size), jnp.bfloat16),
            pltpu.VMEM((depth, columns), jnp.float32),
            pltpu.VMEM((depth, columns), jnp.bfloat16),
            pltpu.VMEM((depth, columns), jnp.bfloat16),
            pltpu.VMEM((8, columns), jnp.int32),
            pltpu.VMEM((half, columns), jnp.float32),
            pltpu.VMEM((total_rows, columns), jnp.float32),
            pltpu.VMEM((rep - 1, half, columns), jnp.float32),
            dma((K_PARTS,)),
            dma((K_PARTS,)),
            dma((rep,)),
            pltpu.SemaphoreType.REGULAR,
            dma((LOADS,)),
            dma((K_PARTS,)),
            dma((3,)),
            dma((rep - 1, N_PARTS)),
            dma((rep - 1, N_PARTS)),
        ],
        compiler_params=pltpu.CompilerParams(
            collective_id=0, has_side_effects=True, vmem_limit_bytes=VMEM_BYTES
        ),
    )(
        *(
            pltpu.with_memory_space_constraint(x, pltpu.HBM)
            for x in (amplitudes, integrals, pair_orbitals, occupied_energy, virtual_energy)
        )
    )


def solution(mesh):
    in_specs = (P("wide", None), P(("wide", "rep"), None), P(None, "wide"), P(), P())
    return jax.shard_map(
        functools.partial(body, mesh.shape["wide"], mesh.shape["rep"]),
        mesh=mesh,
        in_specs=in_specs,
        out_specs=P("rep", "wide"),
        check_vma=False,
    )
```

```python
import functools

import jax
import jax.numpy as jnp
from jax import lax
from jax.experimental import pallas as pl
from jax.experimental.pallas import tpu as pltpu
from jax.sharding import PartitionSpec as P

MESH = pl.DeviceIdType.MESH
LANES = 128
K_PARTS = 1
N_PARTS = 4
DOT = 256
LOADS = 4
VMEM_BYTES = 32 << 20


def split_bf16(x):
    high = x.astype(jnp.bfloat16)
    low = (x - high.astype(jnp.float32)).astype(jnp.bfloat16)
    return high, low


def kernel(
    wide, rep, amp, integ, pairs_in, occ_in, vir_in, out,
    pairs, occ, vir, arrived, rows32, rows16, raw, high, low, index8, scale, part, other,
    send_sem, recv_sem, early_sem, up_sem, in_sem, load_sem, own_sem, small_sem, part_send, part_recv,
):
    w, r = lax.axis_index("wide"), lax.axis_index("rep")
    own_rows, sector_pairs = amp.shape
    depth, columns = integ.shape
    total_rows = own_rows * wide
    half = total_rows // rep
    k_size, n_size, load = depth // K_PARTS, columns // N_PARTS, depth // LOADS

    across = rep - 1 - r
    early = (w > 0) & (r == 0)
    barrier = pltpu.get_barrier_semaphore()

    def signal(sem, chip, core):
        pl.semaphore_signal(
            sem, inc=1, device_id={"wide": chip, "rep": core}, device_id_type=MESH
        )

    signal(barrier, w, across)

    @pl.when(w == 0)
    def _():
        for j in range(1, wide):
            signal(barrier, j, 0)
            signal(barrier, j, rep - 1)

    @pl.when(w > 0)
    def _():
        for d in range(1, wide - 1):
            target = w + d
            signal(barrier, jnp.where(target >= wide, target - wide + 1, target), rep - 1)

    smalls = []
    for i, (source, held) in enumerate(((pairs_in, pairs), (occ_in, occ), (vir_in, vir))):
        smalls.append(pltpu.make_async_copy(source, held, small_sem.at[i]))
        smalls[-1].start()
    loads = []
    for i in range(LOADS):
        rows = pl.ds(i * load, load)
        loads.append(pltpu.make_async_copy(integ.at[rows], raw.at[rows], load_sem.at[i]))

    def load_all():
        for copy in loads:
            copy.start()

    load_all()

    def piece(target, core, k):
        start = pl.multiple_of((target * rep + core) * depth + k * k_size, k_size)
        return amp.at[:, pl.ds(start, k_size)]

    own = []
    for k in range(K_PARTS):
        own.append(pltpu.make_async_copy(piece(w, r, k), arrived.at[k, w], own_sem.at[k]))
        own[-1].start()

    def transfer(target, core, send):
        return pltpu.make_async_remote_copy(
            src_ref=piece(target, core, 0),
            dst_ref=arrived.at[0, w],
            send_sem=send,
            recv_sem=recv_sem.at[0],
            device_id={"wide": target, "rep": core},
            device_id_type=MESH,
        )

    @pl.when(early)
    def _():
        pl.semaphore_wait(barrier, rep + 1)
        for e in range(rep):
            transfer(0, e, early_sem.at[e]).start()
        for e in range(rep):
            signal(in_sem.at[w], 0, e)

    def exchange():
        pl.semaphore_wait(barrier, 1)
        for j in range(1, wide):
            pl.semaphore_wait(in_sem.at[j], 1)
            transfer(j, across, send_sem.at[0]).start()

    def exchange_near():
        @pl.when(early)
        def _():
            pl.semaphore_wait(up_sem, 1)

        @pl.when(jnp.logical_not(early))
        def _():
            pl.semaphore_wait(barrier, (wide - 1) * rep + 1)
            signal(up_sem, w, across)

        for d in range(1, wide - 1):
            target = jnp.where(d < w, d, d + 1)
            transfer(target, across, send_sem.at[0]).start()

    pl.when(jnp.logical_not(2 * w < wide))(exchange_near)

    for copy in smalls:
        copy.wait()
    for s in range(4):
        index8[2 * s : 2 * s + 2, :] = pairs[...]
    occ_count, vir_count = occ.shape[0], vir.shape[0]
    p = r * half + lax.broadcasted_iota(jnp.int32, (half, occ_count), 0)
    lane = lax.broadcasted_iota(jnp.int32, (half, occ_count), 1)
    energies = jnp.broadcast_to(occ[...][None, :], (half, occ_count))
    first = p // occ_count
    occ_sum = jnp.sum(
        jnp.where(lane == first, energies, 0.0), axis=1, keepdims=True
    ) + jnp.sum(
        jnp.where(lane == p - first * occ_count, energies, 0.0), axis=1, keepdims=True
    )
    tables = []
    for t in range(0, vir_count, LANES):
        row = vir[t : min(t + LANES, vir_count)][None, :]
        if row.shape[1] < LANES:
            row = jnp.concatenate([row, jnp.zeros((1, LANES - row.shape[1]), row.dtype)], axis=1)
        tables.append(jnp.broadcast_to(row, (8, LANES)))
    for c in range(0, columns, LANES):
        index = index8[:, c : c + LANES]
        block, slot = index // LANES, index % LANES
        found = jnp.zeros((8, LANES), jnp.float32)
        for t, table in enumerate(tables):
            value = jnp.take_along_axis(table, slot, axis=1)
            found = jnp.where(block == t, value, found)
        vir_sum = found[0:1, :] + found[1:2, :]
        scale[:, c : c + LANES] = 0.5 / (occ_sum - vir_sum)

    def split(i):
        loads[i].wait()
        for j in range(0, load, 16):
            rows = pl.ds(i * load + j, 16)
            h, l = split_bf16(raw[rows, :])
            high[rows, :] = h
            low[rows, :] = l

    for i in range(0):
        split(i)
    pl.when((w > 0) & (2 * w < wide))(exchange_near)
    for i in range(0, LOADS):
        split(i)

    pl.when(w == 0)(exchange)

    others = arrived.at[0, 0 : wide - 1]
    part_copies = []

    def product(k, n):
        ns = pl.ds(n * n_size, n_size)
        total = None
        for c in range(0, k_size, DOT):
            cs = pl.ds(c, DOT)
            ks = pl.ds(k * k_size + c, DOT)
            both = jnp.dot(rows16[:, cs], high[ks, ns], preferred_element_type=jnp.float32)
            cross = jnp.dot(
                rows16[0:total_rows, cs], low[ks, ns], preferred_element_type=jnp.float32
            )
            value = both[0:total_rows] + (both[total_rows:] + cross)
            total = value if total is None else total + value
        return total

    def store(k, n, value):
        ns = pl.ds(n * n_size, n_size)
        if k:
            value = value + part[:, ns]
        part[:, ns] = value
        if k == K_PARTS - 1:
            for e in range(1, rep):
                target = lax.rem(r + e, rep)
                copy = pltpu.make_async_remote_copy(
                    src_ref=part.at[pl.ds(pl.multiple_of(target * half, 8), half), ns],
                    dst_ref=other.at[e - 1, :, ns],
                    send_sem=part_send.at[e - 1, n],
                    recv_sem=part_recv.at[e - 1, n],
                    device_id={"rep": target},
                    device_id_type=MESH,
                )
                copy.start()
                part_copies.append((n, e, copy))

    for k in range(K_PARTS):
        own[k].wait()
        pltpu.make_async_copy(others, others, recv_sem.at[k]).wait()
        for s in range(wide):
            rows32[own_rows * s : own_rows * (s + 1), :] = arrived[k, s]
        h, l = split_bf16(rows32[...])
        rows16[0:total_rows, :] = h
        rows16[total_rows : 2 * total_rows, :] = l
        waiting = None
        for n in range(N_PARTS + 1):
            value = product(k, n) if n < N_PARTS else None
            if n:
                store(k, n - 1, waiting)
            waiting = value

    for k in range(K_PARTS):
        fewer = arrived.at[0, 0 : wide - 2]

        @pl.when(w > 0)
        def _():
            pltpu.make_async_copy(fewer, fewer, send_sem.at[k]).wait()

        @pl.when(w == 0)
        def _():
            pltpu.make_async_copy(others, others, send_sem.at[k]).wait()

    @pl.when(early)
    def _():
        for e in range(rep):
            transfer(0, e, early_sem.at[e]).wait_send()

    for n in range(N_PARTS):
        ns = pl.ds(n * n_size, n_size)
        total = part[pl.ds(pl.multiple_of(r * half, 8), half), ns]
        for m, e, copy in part_copies:
            if m == n:
                copy.wait_recv()
                total = total + other[e - 1, :, ns]
        out[:, ns] = total * scale[:, ns]

    for _, _, copy in part_copies:
        copy.wait_send()


def body(wide, rep, amplitudes, integrals, pair_orbitals, occupied_energy, virtual_energy):
    own_rows = amplitudes.shape[0]
    depth, columns = integrals.shape
    total_rows = own_rows * wide
    half = total_rows // rep
    k_size = depth // K_PARTS
    hbm = pl.BlockSpec(memory_space=pltpu.HBM)
    vmem = pl.BlockSpec(memory_space=pltpu.VMEM)
    dma = pltpu.SemaphoreType.DMA
    return pl.pallas_call(
        functools.partial(kernel, wide, rep),
        out_shape=pltpu.VMEM((half, columns), jnp.float32),
        in_specs=[hbm] * 5,
        out_specs=vmem,
        scratch_shapes=[
            pltpu.VMEM(pair_orbitals.shape, jnp.int32),
            pltpu.VMEM(occupied_energy.shape, jnp.float32),
            pltpu.VMEM(virtual_energy.shape, jnp.float32),
            pltpu.VMEM((K_PARTS, wide, own_rows, k_size), jnp.float32),
            pltpu.VMEM((total_rows, k_size), jnp.float32),
            pltpu.VMEM((2 * total_rows, k_size), jnp.bfloat16),
            pltpu.VMEM((depth, columns), jnp.float32),
            pltpu.VMEM((depth, columns), jnp.bfloat16),
            pltpu.VMEM((depth, columns), jnp.bfloat16),
            pltpu.VMEM((8, columns), jnp.int32),
            pltpu.VMEM((half, columns), jnp.float32),
            pltpu.VMEM((total_rows, columns), jnp.float32),
            pltpu.VMEM((rep - 1, half, columns), jnp.float32),
            dma((K_PARTS,)),
            dma((K_PARTS,)),
            dma((rep,)),
            pltpu.SemaphoreType.REGULAR,
            pltpu.SemaphoreType.REGULAR((wide,)),
            dma((LOADS,)),
            dma((K_PARTS,)),
            dma((3,)),
            dma((rep - 1, N_PARTS)),
            dma((rep - 1, N_PARTS)),
        ],
        compiler_params=pltpu.CompilerParams(
            collective_id=0, has_side_effects=True, vmem_limit_bytes=VMEM_BYTES
        ),
    )(
        *(
            pltpu.with_memory_space_constraint(x, pltpu.HBM)
            for x in (amplitudes, integrals, pair_orbitals, occupied_energy, virtual_energy)
        )
    )


def solution(mesh):
    in_specs = (P("wide", None), P(("wide", "rep"), None), P(None, "wide"), P(), P())
    return jax.shard_map(
        functools.partial(body, mesh.shape["wide"], mesh.shape["rep"]),
        mesh=mesh,
        in_specs=in_specs,
        out_specs=P("rep", "wide"),
        check_vma=False,
    )
```

```python
import functools

import jax
import jax.numpy as jnp
from jax import lax
from jax.experimental import pallas as pl
from jax.experimental.pallas import tpu as pltpu
from jax.sharding import PartitionSpec as P

MESH = pl.DeviceIdType.MESH
LANES = 128
K_PARTS = 1
N_PARTS = 4
DOT = 256
LOADS = 4
VMEM_BYTES = 32 << 20


def split_bf16(x):
    high = x.astype(jnp.bfloat16)
    low = (x - high.astype(jnp.float32)).astype(jnp.bfloat16)
    return high, low


def kernel(
    wide, rep, amp, integ, pairs_in, occ_in, vir_in, out,
    pairs, occ, vir, arrived, rows32, rows16, raw, high, low, index8, scale, part, other,
    send_sem, recv_sem, early_sem, up_sem, in_sem, load_sem, own_sem, small_sem, part_send, part_recv,
):
    w, r = lax.axis_index("wide"), lax.axis_index("rep")
    own_rows, sector_pairs = amp.shape
    depth, columns = integ.shape
    total_rows = own_rows * wide
    half = total_rows // rep
    k_size, n_size, load = depth // K_PARTS, columns // N_PARTS, depth // LOADS

    across = rep - 1 - r
    early = (w > 0) & (r == 0)
    barrier = pltpu.get_barrier_semaphore()

    def signal(sem, chip, core):
        pl.semaphore_signal(
            sem, inc=1, device_id={"wide": chip, "rep": core}, device_id_type=MESH
        )

    signal(barrier, w, across)

    @pl.when(w == 0)
    def _():
        for j in range(1, wide):
            signal(barrier, j, 0)
            signal(barrier, j, rep - 1)

    @pl.when(w > 0)
    def _():
        for d in range(1, wide - 1):
            target = w + d
            signal(barrier, jnp.where(target >= wide, target - wide + 1, target), rep - 1)

    def piece(target, core, k):
        start = pl.multiple_of((target * rep + core) * depth + k * k_size, k_size)
        return amp.at[:, pl.ds(start, k_size)]

    def transfer(target, core, send):
        return pltpu.make_async_remote_copy(
            src_ref=piece(target, core, 0),
            dst_ref=arrived.at[0, w],
            send_sem=send,
            recv_sem=recv_sem.at[0],
            device_id={"wide": target, "rep": core},
            device_id_type=MESH,
        )

    @pl.when(early)
    def _():
        pl.semaphore_wait(barrier, rep + 1)
        for e in range(rep):
            transfer(0, e, early_sem.at[e]).start()
        for e in range(rep):
            signal(in_sem.at[w], 0, e)

    smalls = []
    for i, (source, held) in enumerate(((pairs_in, pairs), (occ_in, occ), (vir_in, vir))):
        smalls.append(pltpu.make_async_copy(source, held, small_sem.at[i]))
        smalls[-1].start()
    loads = []
    for i in range(LOADS):
        rows = pl.ds(i * load, load)
        loads.append(pltpu.make_async_copy(integ.at[rows], raw.at[rows], load_sem.at[i]))

    def load_all():
        for copy in loads:
            copy.start()

    load_all()

    own = []
    for k in range(K_PARTS):
        own.append(pltpu.make_async_copy(piece(w, r, k), arrived.at[k, w], own_sem.at[k]))
        own[-1].start()

    def exchange():
        pl.semaphore_wait(barrier, 1)
        for j in range(1, wide):
            pl.semaphore_wait(in_sem.at[j], 1)
            transfer(j, across, send_sem.at[0]).start()

    def exchange_near():
        @pl.when(early)
        def _():
            pl.semaphore_wait(up_sem, 1)

        @pl.when(jnp.logical_not(early))
        def _():
            pl.semaphore_wait(barrier, (wide - 1) * rep + 1)
            signal(up_sem, w, across)

        for d in range(1, wide - 1):
            target = jnp.where(d < w, d, d + 1)
            transfer(target, across, send_sem.at[0]).start()

    pl.when(jnp.logical_not(2 * w < wide))(exchange_near)

    for copy in smalls:
        copy.wait()
    for s in range(4):
        index8[2 * s : 2 * s + 2, :] = pairs[...]
    occ_count, vir_count = occ.shape[0], vir.shape[0]
    p = r * half + lax.broadcasted_iota(jnp.int32, (half, occ_count), 0)
    lane = lax.broadcasted_iota(jnp.int32, (half, occ_count), 1)
    energies = jnp.broadcast_to(occ[...][None, :], (half, occ_count))
    first = p // occ_count
    occ_sum = jnp.sum(
        jnp.where(lane == first, energies, 0.0), axis=1, keepdims=True
    ) + jnp.sum(
        jnp.where(lane == p - first * occ_count, energies, 0.0), axis=1, keepdims=True
    )
    tables = []
    for t in range(0, vir_count, LANES):
        row = vir[t : min(t + LANES, vir_count)][None, :]
        if row.shape[1] < LANES:
            row = jnp.concatenate([row, jnp.zeros((1, LANES - row.shape[1]), row.dtype)], axis=1)
        tables.append(jnp.broadcast_to(row, (8, LANES)))
    for c in range(0, columns, LANES):
        index = index8[:, c : c + LANES]
        block, slot = index // LANES, index % LANES
        found = jnp.zeros((8, LANES), jnp.float32)
        for t, table in enumerate(tables):
            value = jnp.take_along_axis(table, slot, axis=1)
            found = jnp.where(block == t, value, found)
        vir_sum = found[0:1, :] + found[1:2, :]
        scale[:, c : c + LANES] = 0.5 / (occ_sum - vir_sum)

    def split(i):
        loads[i].wait()
        for j in range(0, load, 16):
            rows = pl.ds(i * load + j, 16)
            h, l = split_bf16(raw[rows, :])
            high[rows, :] = h
            low[rows, :] = l

    for i in range(0):
        split(i)
    pl.when((w > 0) & (2 * w < wide))(exchange_near)
    for i in range(0, LOADS):
        split(i)

    pl.when(w == 0)(exchange)

    others = arrived.at[0, 0 : wide - 1]
    part_copies = []

    def product(k, n):
        ns = pl.ds(n * n_size, n_size)
        total = None
        for c in range(0, k_size, DOT):
            cs = pl.ds(c, DOT)
            ks = pl.ds(k * k_size + c, DOT)
            both = jnp.dot(rows16[:, cs], high[ks, ns], preferred_element_type=jnp.float32)
            cross = jnp.dot(
                rows16[0:total_rows, cs], low[ks, ns], preferred_element_type=jnp.float32
            )
            value = both[0:total_rows] + (both[total_rows:] + cross)
            total = value if total is None else total + value
        return total

    def store(k, n, value):
        ns = pl.ds(n * n_size, n_size)
        if k:
            value = value + part[:, ns]
        part[:, ns] = value
        if k == K_PARTS - 1:
            for e in range(1, rep):
                target = lax.rem(r + e, rep)
                copy = pltpu.make_async_remote_copy(
                    src_ref=part.at[pl.ds(pl.multiple_of(target * half, 8), half), ns],
                    dst_ref=other.at[e - 1, :, ns],
                    send_sem=part_send.at[e - 1, n],
                    recv_sem=part_recv.at[e - 1, n],
                    device_id={"rep": target},
                    device_id_type=MESH,
                )
                copy.start()
                part_copies.append((n, e, copy))

    for k in range(K_PARTS):
        own[k].wait()
        pltpu.make_async_copy(others, others, recv_sem.at[k]).wait()
        h, l = split_bf16(arrived[k].reshape(total_rows, k_size))
        rows16[0:total_rows, :] = h
        rows16[total_rows : 2 * total_rows, :] = l
        waiting = None
        for n in range(N_PARTS + 1):
            value = product(k, n) if n < N_PARTS else None
            if n:
                store(k, n - 1, waiting)
            waiting = value

    for k in range(K_PARTS):
        fewer = arrived.at[0, 0 : wide - 2]

        @pl.when(w > 0)
        def _():
            pltpu.make_async_copy(fewer, fewer, send_sem.at[k]).wait()

        @pl.when(w == 0)
        def _():
            pltpu.make_async_copy(others, others, send_sem.at[k]).wait()

    @pl.when(early)
    def _():
        for e in range(rep):
            transfer(0, e, early_sem.at[e]).wait_send()

    for n in range(N_PARTS):
        ns = pl.ds(n * n_size, n_size)
        total = part[pl.ds(pl.multiple_of(r * half, 8), half), ns]
        for m, e, copy in part_copies:
            if m == n:
                copy.wait_recv()
                total = total + other[e - 1, :, ns]
        out[:, ns] = total * scale[:, ns]

    for _, _, copy in part_copies:
        copy.wait_send()


def body(wide, rep, amplitudes, integrals, pair_orbitals, occupied_energy, virtual_energy):
    own_rows = amplitudes.shape[0]
    depth, columns = integrals.shape
    total_rows = own_rows * wide
    half = total_rows // rep
    k_size = depth // K_PARTS
    hbm = pl.BlockSpec(memory_space=pltpu.HBM)
    vmem = pl.BlockSpec(memory_space=pltpu.VMEM)
    dma = pltpu.SemaphoreType.DMA
    return pl.pallas_call(
        functools.partial(kernel, wide, rep),
        out_shape=pltpu.VMEM((half, columns), jnp.float32),
        in_specs=[hbm] * 5,
        out_specs=vmem,
        scratch_shapes=[
            pltpu.VMEM(pair_orbitals.shape, jnp.int32),
            pltpu.VMEM(occupied_energy.shape, jnp.float32),
            pltpu.VMEM(virtual_energy.shape, jnp.float32),
            pltpu.VMEM((K_PARTS, wide, own_rows, k_size), jnp.float32),
            pltpu.VMEM((total_rows, k_size), jnp.float32),
            pltpu.VMEM((2 * total_rows, k_size), jnp.bfloat16),
            pltpu.VMEM((depth, columns), jnp.float32),
            pltpu.VMEM((depth, columns), jnp.bfloat16),
            pltpu.VMEM((depth, columns), jnp.bfloat16),
            pltpu.VMEM((8, columns), jnp.int32),
            pltpu.VMEM((half, columns), jnp.float32),
            pltpu.VMEM((total_rows, columns), jnp.float32),
            pltpu.VMEM((rep - 1, half, columns), jnp.float32),
            dma((K_PARTS,)),
            dma((K_PARTS,)),
            dma((rep,)),
            pltpu.SemaphoreType.REGULAR,
            pltpu.SemaphoreType.REGULAR((wide,)),
            dma((LOADS,)),
            dma((K_PARTS,)),
            dma((3,)),
            dma((rep - 1, N_PARTS)),
            dma((rep - 1, N_PARTS)),
        ],
        compiler_params=pltpu.CompilerParams(
            collective_id=0, has_side_effects=True, vmem_limit_bytes=VMEM_BYTES
        ),
    )(
        *(
            pltpu.with_memory_space_constraint(x, pltpu.HBM)
            for x in (amplitudes, integrals, pair_orbitals, occupied_energy, virtual_energy)
        )
    )


def solution(mesh):
    in_specs = (P("wide", None), P(("wide", "rep"), None), P(None, "wide"), P(), P())
    return jax.shard_map(
        functools.partial(body, mesh.shape["wide"], mesh.shape["rep"]),
        mesh=mesh,
        in_specs=in_specs,
        out_specs=P("rep", "wide"),
        check_vma=False,
    )
```

```python
import functools

import jax
import jax.numpy as jnp
from jax import lax
from jax.experimental import pallas as pl
from jax.experimental.pallas import tpu as pltpu
from jax.sharding import PartitionSpec as P

MESH = pl.DeviceIdType.MESH
LANES = 128
K_PARTS = 1
N_PARTS = 4
DOT = 256
LOADS = 4
VMEM_BYTES = 32 << 20


def split_bf16(x):
    high = x.astype(jnp.bfloat16)
    low = (x - high.astype(jnp.float32)).astype(jnp.bfloat16)
    return high, low


def kernel(
    wide, rep, amp, integ, pairs_in, occ_in, vir_in, out,
    pairs, occ, vir, amps, arrived, rows32, rows16, raw, high, low, index8, scale, part, other,
    send_sem, recv_sem, early_sem, up_sem, in_sem, amp_sem, load_sem, own_sem, small_sem, part_send, part_recv,
):
    w, r = lax.axis_index("wide"), lax.axis_index("rep")
    own_rows, sector_pairs = amp.shape
    depth, columns = integ.shape
    total_rows = own_rows * wide
    half = total_rows // rep
    k_size, n_size, load = depth // K_PARTS, columns // N_PARTS, depth // LOADS

    across = rep - 1 - r
    early = (w > 0) & (r == 0)
    barrier = pltpu.get_barrier_semaphore()

    def signal(sem, chip, core):
        pl.semaphore_signal(
            sem, inc=1, device_id={"wide": chip, "rep": core}, device_id_type=MESH
        )

    signal(barrier, w, across)

    @pl.when(w == 0)
    def _():
        for j in range(1, wide):
            signal(barrier, j, 0)
            signal(barrier, j, rep - 1)

    @pl.when(w > 0)
    def _():
        for d in range(1, wide - 1):
            target = w + d
            signal(barrier, jnp.where(target >= wide, target - wide + 1, target), rep - 1)

    smalls = []
    for i, (source, held) in enumerate(((pairs_in, pairs), (occ_in, occ), (vir_in, vir))):
        smalls.append(pltpu.make_async_copy(source, held, small_sem.at[i]))
        smalls[-1].start()
    loads = []
    for i in range(LOADS):
        rows = pl.ds(i * load, load)
        loads.append(pltpu.make_async_copy(integ.at[rows], raw.at[rows], load_sem.at[i]))

    def load_all():
        for copy in loads:
            copy.start()

    load_all()
    amp_load = pltpu.make_async_copy(amp, amps, amp_sem)
    pl.when(2 * w < wide)(amp_load.start)

    def piece(target, core, k, held=amp):
        start = pl.multiple_of((target * rep + core) * depth + k * k_size, k_size)
        return held.at[:, pl.ds(start, k_size)]

    own = []
    for k in range(K_PARTS):
        own.append(pltpu.make_async_copy(piece(w, r, k), arrived.at[k, w], own_sem.at[k]))
        own[-1].start()

    def transfer(target, core, send, held=amp):
        return pltpu.make_async_remote_copy(
            src_ref=piece(target, core, 0, held),
            dst_ref=arrived.at[0, w],
            send_sem=send,
            recv_sem=recv_sem.at[0],
            device_id={"wide": target, "rep": core},
            device_id_type=MESH,
        )

    @pl.when(early)
    def _():
        pl.semaphore_wait(barrier, rep + 1)
        for e in range(rep):
            transfer(0, e, early_sem.at[e]).start()
        for e in range(rep):
            signal(in_sem.at[w], 0, e)

    def exchange():
        pl.semaphore_wait(barrier, 1)
        for j in range(1, wide):
            pl.semaphore_wait(in_sem.at[j], 1)
            transfer(j, across, send_sem.at[0], amps).start()

    def exchange_near(held=amp):
        @pl.when(early)
        def _():
            pl.semaphore_wait(up_sem, 1)

        @pl.when(jnp.logical_not(early))
        def _():
            pl.semaphore_wait(barrier, (wide - 1) * rep + 1)
            signal(up_sem, w, across)

        for d in range(1, wide - 1):
            target = jnp.where(d < w, d, d + 1)
            transfer(target, across, send_sem.at[0], held).start()

    pl.when(jnp.logical_not(2 * w < wide))(exchange_near)

    for copy in smalls:
        copy.wait()
    for s in range(4):
        index8[2 * s : 2 * s + 2, :] = pairs[...]
    occ_count, vir_count = occ.shape[0], vir.shape[0]
    p = r * half + lax.broadcasted_iota(jnp.int32, (half, occ_count), 0)
    lane = lax.broadcasted_iota(jnp.int32, (half, occ_count), 1)
    energies = jnp.broadcast_to(occ[...][None, :], (half, occ_count))
    first = p // occ_count
    occ_sum = jnp.sum(
        jnp.where(lane == first, energies, 0.0), axis=1, keepdims=True
    ) + jnp.sum(
        jnp.where(lane == p - first * occ_count, energies, 0.0), axis=1, keepdims=True
    )
    tables = []
    for t in range(0, vir_count, LANES):
        row = vir[t : min(t + LANES, vir_count)][None, :]
        if row.shape[1] < LANES:
            row = jnp.concatenate([row, jnp.zeros((1, LANES - row.shape[1]), row.dtype)], axis=1)
        tables.append(jnp.broadcast_to(row, (8, LANES)))
    for c in range(0, columns, LANES):
        index = index8[:, c : c + LANES]
        block, slot = index // LANES, index % LANES
        found = jnp.zeros((8, LANES), jnp.float32)
        for t, table in enumerate(tables):
            value = jnp.take_along_axis(table, slot, axis=1)
            found = jnp.where(block == t, value, found)
        vir_sum = found[0:1, :] + found[1:2, :]
        scale[:, c : c + LANES] = 0.5 / (occ_sum - vir_sum)

    def split(i):
        loads[i].wait()
        for j in range(0, load, 16):
            rows = pl.ds(i * load + j, 16)
            h, l = split_bf16(raw[rows, :])
            high[rows, :] = h
            low[rows, :] = l

    for i in range(0):
        split(i)
    pl.when(2 * w < wide)(amp_load.wait)
    pl.when((w > 0) & (2 * w < wide))(lambda: exchange_near(amps))
    for i in range(0, LOADS):
        split(i)

    pl.when(w == 0)(exchange)

    others = arrived.at[0, 0 : wide - 1]
    part_copies = []

    def product(k, n):
        ns = pl.ds(n * n_size, n_size)
        total = None
        for c in range(0, k_size, DOT):
            cs = pl.ds(c, DOT)
            ks = pl.ds(k * k_size + c, DOT)
            both = jnp.dot(rows16[:, cs], high[ks, ns], preferred_element_type=jnp.float32)
            cross = jnp.dot(
                rows16[0:total_rows, cs], low[ks, ns], preferred_element_type=jnp.float32
            )
            value = both[0:total_rows] + (both[total_rows:] + cross)
            total = value if total is None else total + value
        return total

    def store(k, n, value):
        ns = pl.ds(n * n_size, n_size)
        if k:
            value = value + part[:, ns]
        part[:, ns] = value
        if k == K_PARTS - 1:
            for e in range(1, rep):
                target = lax.rem(r + e, rep)
                copy = pltpu.make_async_remote_copy(
                    src_ref=part.at[pl.ds(pl.multiple_of(target * half, 8), half), ns],
                    dst_ref=other.at[e - 1, :, ns],
                    send_sem=part_send.at[e - 1, n],
                    recv_sem=part_recv.at[e - 1, n],
                    device_id={"rep": target},
                    device_id_type=MESH,
                )
                copy.start()
                part_copies.append((n, e, copy))

    for k in range(K_PARTS):
        own[k].wait()
        pltpu.make_async_copy(others, others, recv_sem.at[k]).wait()
        for s in range(wide):
            rows32[own_rows * s : own_rows * (s + 1), :] = arrived[k, s]
        h, l = split_bf16(rows32[...])
        rows16[0:total_rows, :] = h
        rows16[total_rows : 2 * total_rows, :] = l
        waiting = None
        for n in range(N_PARTS + 1):
            value = product(k, n) if n < N_PARTS else None
            if n:
                store(k, n - 1, waiting)
            waiting = value

    for k in range(K_PARTS):
        fewer = arrived.at[0, 0 : wide - 2]

        @pl.when(w > 0)
        def _():
            pltpu.make_async_copy(fewer, fewer, send_sem.at[k]).wait()

        @pl.when(w == 0)
        def _():
            pltpu.make_async_copy(others, others, send_sem.at[k]).wait()

    @pl.when(early)
    def _():
        for e in range(rep):
            transfer(0, e, early_sem.at[e]).wait_send()

    for n in range(N_PARTS):
        ns = pl.ds(n * n_size, n_size)
        total = part[pl.ds(pl.multiple_of(r * half, 8), half), ns]
        for m, e, copy in part_copies:
            if m == n:
                copy.wait_recv()
                total = total + other[e - 1, :, ns]
        out[:, ns] = total * scale[:, ns]

    for _, _, copy in part_copies:
        copy.wait_send()


def body(wide, rep, amplitudes, integrals, pair_orbitals, occupied_energy, virtual_energy):
    own_rows = amplitudes.shape[0]
    depth, columns = integrals.shape
    total_rows = own_rows * wide
    half = total_rows // rep
    k_size = depth // K_PARTS
    hbm = pl.BlockSpec(memory_space=pltpu.HBM)
    vmem = pl.BlockSpec(memory_space=pltpu.VMEM)
    dma = pltpu.SemaphoreType.DMA
    return pl.pallas_call(
        functools.partial(kernel, wide, rep),
        out_shape=pltpu.VMEM((half, columns), jnp.float32),
        in_specs=[hbm] * 5,
        out_specs=vmem,
        scratch_shapes=[
            pltpu.VMEM(pair_orbitals.shape, jnp.int32),
            pltpu.VMEM(occupied_energy.shape, jnp.float32),
            pltpu.VMEM(virtual_energy.shape, jnp.float32),
            pltpu.VMEM(amplitudes.shape, jnp.float32),
            pltpu.VMEM((K_PARTS, wide, own_rows, k_size), jnp.float32),
            pltpu.VMEM((total_rows, k_size), jnp.float32),
            pltpu.VMEM((2 * total_rows, k_size), jnp.bfloat16),
            pltpu.VMEM((depth, columns), jnp.float32),
            pltpu.VMEM((depth, columns), jnp.bfloat16),
            pltpu.VMEM((depth, columns), jnp.bfloat16),
            pltpu.VMEM((8, columns), jnp.int32),
            pltpu.VMEM((half, columns), jnp.float32),
            pltpu.VMEM((total_rows, columns), jnp.float32),
            pltpu.VMEM((rep - 1, half, columns), jnp.float32),
            dma((K_PARTS,)),
            dma((K_PARTS,)),
            dma((rep,)),
            pltpu.SemaphoreType.REGULAR,
            pltpu.SemaphoreType.REGULAR((wide,)),
            dma,
            dma((LOADS,)),
            dma((K_PARTS,)),
            dma((3,)),
            dma((rep - 1, N_PARTS)),
            dma((rep - 1, N_PARTS)),
        ],
        compiler_params=pltpu.CompilerParams(
            collective_id=0, has_side_effects=True, vmem_limit_bytes=VMEM_BYTES
        ),
    )(
        *(
            pltpu.with_memory_space_constraint(x, pltpu.HBM)
            for x in (amplitudes, integrals, pair_orbitals, occupied_energy, virtual_energy)
        )
    )


def solution(mesh):
    in_specs = (P("wide", None), P(("wide", "rep"), None), P(None, "wide"), P(), P())
    return jax.shard_map(
        functools.partial(body, mesh.shape["wide"], mesh.shape["rep"]),
        mesh=mesh,
        in_specs=in_specs,
        out_specs=P("rep", "wide"),
        check_vma=False,
    )
```
